256 devices in a mesh: row: 32 (over y, z_lo, x), col: 8 (over z_hi, core).
Axes of the slice: x: 4, y: 4, z: 8 (z_hi: 4, z_lo: 2; z = z_hi * 2 + z_lo), core: 2. Of those that a mesh axis runs over, the one named last changes fastest.
Arguments:
- p_cov: float32 [8192, 8192], P('row', 'col'), as said below
- a_blocks: float32 [64, 16, 128, 128], P('row'), may hold values from -0.15625 to 0.15625
- pattern: int32 [64, 16], P('row'), may hold values from -1 to 63, as said below
- q_diag: float32 [8192], P('row'), may hold values from 0.2 to 2
Outputs:
- p_next: float32 [8192, 8192], P('row', 'col')
The draws below stay inside these ranges and needn't reach their ends.
Inputs may be any that keep to these rules, and one draw needn't show every extreme that they name: p_cov is exactly symmetric. `pattern`: in each row i the entries that are not -1 are distinct, lie within 8 of i, include i itself and fill the leading slots; some row uses all 16 slots.
All inputs are finite; a program needn't handle non-finite values.
Results may differ from the reference program's by a relative error of at most 0.0003.
Values sent between devices are 32-bit elements; how exact they have to be, the bound alone decides.
A program may use at most 64 MiB of HBM per device.

```python
import math
import jax
import jax.numpy as jnp
from jax import lax

NB = 64
BS = 128
KMAX = 16
REACH = 8
N = 8192


def draw_p_cov(key, part):
    order = NB * BS
    key_normal = jax.random.fold_in(jax.random.fold_in(key, 7), 0)
    raw = jax.random.normal(key_normal, (order, order), jnp.float32)
    symmetric = 0.5 * (raw + raw.T)
    return symmetric + 2.0 * jnp.eye(order, dtype=jnp.float32)


def draw_pattern(key, part):
    key_score, key_count, key_full = jax.random.split(jax.random.fold_in(key, 11), 3)
    width = 2 * REACH + 1
    row_ids = jnp.arange(NB, dtype=jnp.int32)[:, None]
    offsets = jnp.arange(width, dtype=jnp.int32)[None, :] - REACH
    candidate = row_ids + offsets
    valid = (candidate >= 0) & (candidate < NB)
    scores = jax.random.randint(key_score, (NB, width), 0, 1 << 20) * 64 + jnp.arange(width, dtype=jnp.int32)[None, :]
    scores = jnp.where(offsets == 0, -1, scores)
    scores = jnp.where(valid, scores, 1 << 29)
    unused, order_idx = jax.lax.top_k(-scores, KMAX)
    counts = jax.random.randint(key_count, (NB,), KMAX // 2, KMAX + 1)
    full_row = jax.random.randint(key_full, (), REACH, NB - REACH)
    counts = jnp.where(jnp.arange(NB, dtype=jnp.int32) == full_row, KMAX, counts)
    chosen_off = jnp.take(offsets[0], order_idx)
    chosen = row_ids + chosen_off
    chosen_ok = jnp.take_along_axis(valid, order_idx, axis=1)
    slot_ids = jnp.arange(KMAX, dtype=jnp.int32)[None, :]
    keep = (slot_ids < counts[:, None]) & chosen_ok
    return jnp.where(keep, chosen, -1).astype(jnp.int32)


def block_levels(stream_key, extent, cuts, low, high):
    factor_of, own = 1.0, jax.random.fold_in(stream_key, 6)
    for position, parts in cuts:
        steps = jnp.exp(jax.random.uniform(jax.random.fold_in(own, position), (parts,), jnp.float32, low / len(cuts), high / len(cuts)))
        factor_of = factor_of * jnp.repeat(steps, extent[position] // parts).reshape([-1 if axis == position else 1 for axis in range(len(extent))])
    return factor_of


def centred(own_key, extent, scale, reach, pieces=(), held_as=jnp.bfloat16):
    entries = scale * jax.random.normal(own_key, extent, jnp.float32)
    if pieces:
        entries = entries * block_levels(own_key, extent, pieces, -0.22, 0.18)
    return jnp.clip(entries, -reach, reach).astype(held_as)


def setup_inputs(seed: int = 0) -> dict:
    key_list = jax.random.split(jax.random.key(seed), 5)
    return {
        "p_cov": draw_p_cov(jax.random.fold_in(key_list[4], 71), 0),
        "a_blocks": centred(key_list[1], (NB, KMAX, BS, BS), (BS * 12) ** -0.5, 0.15625, ((0, 32),), jnp.float32),
        "pattern": draw_pattern(jax.random.fold_in(key_list[4], 71), 0),
        "q_diag": jnp.clip(jnp.exp(math.log(2.0) - 2.3025851 * jax.random.uniform(key_list[3], (N,), jnp.float32) ** block_levels(key_list[3], (N,), ((0, 32),), -0.2, 0.2)), 0.2, 2.0),
    }


time_step = 0.25


def apply_jacobian(p_full, a_blocks, pattern):
    stacked = p_full.reshape(NB, BS, NB * BS)

    def one_row(index):
        slots = pattern[index]
        safe = jnp.clip(slots, 0, NB - 1).astype(jnp.int32)
        picked = stacked[safe]
        weights = a_blocks[index] * (slots >= 0).astype(a_blocks.dtype)[:, None, None]
        return jnp.einsum("sxy,syn->xn", weights, picked, precision=lax.Precision.HIGHEST)

    return lax.map(one_row, jnp.arange(NB, dtype=jnp.int32)).reshape(NB * BS, NB * BS)


def reference(p_cov, a_blocks, pattern, q_diag):
    noise = jnp.diag(q_diag)

    def tendency(p_full):
        product = apply_jacobian(p_full, a_blocks, pattern)
        return product + product.T + noise

    k_first = tendency(p_cov)
    p_mid = p_cov + time_step * k_first
    k_second = tendency(p_mid)
    return p_cov + (0.5 * time_step) * (k_first + k_second)
```

```python
import jax
import jax.numpy as jnp
from jax import lax
from jax.experimental import pallas as pl
from jax.experimental.pallas import tpu as pltpu
from jax.sharding import PartitionSpec as P

BS = 128
REACH = 8
WIDTH = 2 * REACH + 1
HALF = 256
TILE = 512
SPAN = (WIDTH + 1) * BS
MESH = pl.DeviceIdType.MESH
F32 = jnp.float32
BF16 = jnp.bfloat16

S_RELAYOUT, S_NOISE, S_BAND, S_FWD, S_HALO, S_MIRROR, S_BACK, N_SEND = 0, 4, 6, 10, 11, 27, 31, 35
R_RELAYOUT, R_NOISE, R_BAND, R_HALO, R_MIRROR, R_BACK, N_RECV = 0, 4, 6, 10, 26, 30, 34


def kernel(
    slot_ref, p_ref, a_ref, q_ref, o_ref,
    band, band_hi, band_lo, ext_p, ext_k, ext_hi, ext_lo,
    first, first_t, total, total_t, result, noise, send, recv,
):
    row = lax.axis_index("row")
    col = lax.axis_index("col")
    x, z0, y = row % 4, (row // 4) % 2, row // 8
    core, zh = col % 2, col // 2
    tile_i, tile_j = 4 * y + 2 * z0 + core, 4 * zh + x

    def device(x, y, z0, zh, core):
        return (8 * y + 4 * z0 + x, 2 * zh + core)

    def remote(src, dst, target, s, r):
        return pltpu.make_async_remote_copy(
            src_ref=src, dst_ref=dst, send_sem=send.at[s], recv_sem=recv.at[r],
            device_id=target, device_id_type=MESH,
        )

    pending = []

    def start(src, dst, target, s, r, local=None):
        copy = remote(src, dst, target, s, r)
        if local is None:
            copy.start()
            pending.append((None, copy))
            return
        pl.when(jnp.logical_not(local))(copy.start)
        pl.when(local)(pltpu.make_async_copy(src, dst, recv.at[r]).start)
        pending.append((jnp.logical_not(local), copy))

    def arrived(dst, r):
        remote(dst, dst, (row, col), 0, r).wait_recv()

    partner = device(x, y, z0, zh, 1 - core)

    mine = x // 2 == core
    part = x % 2
    for h in range(2):
        target = device(2 * core + h, y, z0, zh, x // 2)
        local = jnp.logical_and(mine, part == h)
        start(q_ref, noise.at[part], target, S_NOISE + h, R_NOISE + part, local)
    for cc in range(2):
        for h in range(2):
            target = device(2 * core + h, y, z0, zh, x // 2)
            local = jnp.logical_and(mine, part == h)
            start(
                p_ref.at[:, pl.ds(TILE * h + HALF * cc, HALF)],
                ext_p.at[cc, pl.ds(pl.multiple_of(2 * TILE + HALF * part, HALF), HALF), :],
                target, S_RELAYOUT + 2 * cc + h, R_RELAYOUT + 2 * cc + part, local,
            )

    def right(x):
        return (x + 1) % 4

    def left(x):
        return (x + 3) % 4

    @pl.when(mine)
    def _():
        for b in range(2):
            for d in range(WIDTH):
                slot = slot_ref[b, d]
                block = a_ref[b, jnp.maximum(slot, 0)]
                band[part, b, :, d * BS:(d + 1) * BS] = jnp.where(slot >= 0, block, 0.0)
        for t, b in enumerate((0, 1)):
            remote(band.at[part, b], band.at[part, b], device(right(x), y, z0, zh, core),
                   S_BAND + t, R_BAND + 2 * part + b).start()
            remote(band.at[part, 1 - b], band.at[part, 1 - b], device(left(x), y, z0, zh, core),
                   S_BAND + 2 + t, R_BAND + 2 * part + 1 - b).start()

    step = (x + 4 - 2 * core) % 4
    fwd_c = 1 - step % 2
    fwd_right = jnp.logical_or(step == 1, step == 2)
    fwd_b = jnp.where(fwd_right, 0, 1)
    fwd_x = jnp.where(fwd_right, right(x), left(x))

    def forward_band():
        unit = band.at[fwd_c, fwd_b]
        arrived(unit, R_BAND + 2 * fwd_c + fwd_b)
        start(unit, unit, device(fwd_x, y, z0, zh, core), S_FWD, R_BAND + 2 * fwd_c + fwd_b)

    d_slot = jnp.where(z0 == 0, 4, 0)
    y_slot = 4 - d_slot
    y_next = jnp.where(z0 == 0, (y + 1) % 4, (y + 3) % 4)
    near = jnp.where(core == 0, 1, 3)
    f_slot = jnp.where(core == 0, 4, 0)
    f_dst = jnp.where(core == 0, 3, 1)
    f_from_z = f_slot == d_slot

    def halo(ext, base):
        def at(cc, slot):
            return ext.at[cc, pl.ds(pl.multiple_of(slot * TILE, TILE), TILE), :]

        def sem(kind, cc):
            return 8 * base + 2 * kind + cc

        def own(cc):
            start(at(cc, 2), at(cc, y_slot), device(x, y, 1 - z0, zh, core),
                  S_HALO + sem(0, cc), R_HALO + sem(0, cc))
            start(at(cc, 2), at(cc, near), partner, S_HALO + sem(1, cc), R_HALO + sem(1, cc))

        def across(cc):
            start(at(cc, f_slot), at(cc, f_dst), partner,
                  S_HALO + sem(3, cc), R_HALO + sem(3, cc))

        def from_z(cc):
            arrived(at(cc, d_slot), R_HALO + sem(0, cc))
            start(at(cc, d_slot), at(cc, y_slot), device(x, y_next, z0, zh, core),
                  S_HALO + sem(2, cc), R_HALO + sem(2, cc))
            pl.when(f_from_z)(lambda: remote(
                at(cc, f_slot), at(cc, f_dst), partner,
                S_HALO + sem(3, cc), R_HALO + sem(3, cc)).start())

        def from_y(cc):
            arrived(at(cc, y_slot), R_HALO + sem(2, cc))
            pl.when(jnp.logical_not(f_from_z))(lambda: remote(
                at(cc, f_slot), at(cc, f_dst), partner,
                S_HALO + sem(3, cc), R_HALO + sem(3, cc)).start())
            pending.append((None, remote(
                at(cc, f_slot), at(cc, f_dst), partner,
                S_HALO + sem(3, cc), R_HALO + sem(3, cc))))

        def rest(cc):
            arrived(at(cc, 4 - near), R_HALO + sem(1, cc))
            arrived(at(cc, 4 - f_dst), R_HALO + sem(3, cc))

        return own, from_z, from_y, rest

    def split(ext, cc):
        def piece(n, _):
            rows = pl.ds(pl.multiple_of(n * BS, BS), BS)
            value = ext[cc, rows, :]
            hi = value.astype(BF16)
            ext_hi[cc, rows, :] = hi
            ext_lo[cc, rows, :] = (value - hi.astype(F32)).astype(BF16)
            return 0
        lax.fori_loop(0, 5 * TILE // BS, piece, 0)

    def product(c, cc):
        rows = slice(HALF * c, HALF * c + SPAN)
        hi, lo = ext_hi[cc, rows, :], ext_lo[cc, rows, :]
        acc = jnp.dot(band_hi[c], hi, preferred_element_type=F32)
        acc += jnp.dot(band_hi[c], lo, preferred_element_type=F32)
        acc += jnp.dot(band_lo[c], hi, preferred_element_type=F32)
        return acc

    def split_band(c):
        for b in range(2):
            empty = slice(0, BS) if b else slice(WIDTH * BS, SPAN)
            rows = slice(b * BS, (b + 1) * BS)
            band_hi[c, rows, empty] = jnp.zeros((BS, BS), BF16)
            band_lo[c, rows, empty] = jnp.zeros((BS, BS), BF16)
            for d in range(WIDTH):
                value = band[c, b, :, d * BS:(d + 1) * BS]
                hi = value.astype(BF16)
                cols = slice((b + d) * BS, (b + d + 1) * BS)
                band_hi[c, rows, cols] = hi
                band_lo[c, rows, cols] = (value - hi.astype(F32)).astype(BF16)

    mirror = device(2 * z0 + core, zh, x // 2, y, x % 2)
    on_diagonal = tile_i == tile_j
    eye = (
        lax.broadcasted_iota(jnp.int32, (HALF, HALF), 0)
        == lax.broadcasted_iota(jnp.int32, (HALF, HALF), 1)
    )

    def diagonal(c):
        values = jnp.broadcast_to(noise[c, 0:1, :], (HALF, HALF))
        return jnp.where(jnp.logical_and(eye, on_diagonal), values, 0.0)

    own, from_z, from_y, rest = halo(ext_p, 0)
    for cc in range(2):
        for c in range(2):
            arrived(ext_p.at[cc, pl.ds(2 * TILE + HALF * c, HALF), :], R_RELAYOUT + 2 * cc + c)
        own(cc)
    from_z(0)
    from_z(1)
    from_y(0)
    from_y(1)
    forward_band()
    for cc in range(2):
        rest(cc)
        split(ext_p, cc)
    for c in range(2):
        arrived(noise.at[c], R_NOISE + c)

    for c in range(2):
        for b in range(2):
            seen = jnp.logical_and(fwd_c == c, fwd_b == b)
            held = jnp.logical_and(mine, part == c)
            skip = jnp.logical_or(seen, held)
            pl.when(jnp.logical_not(skip))(
                lambda c=c, b=b: arrived(band.at[c, b], R_BAND + 2 * c + b))
        split_band(c)
        for cc in range(2):
            first[c, cc] = product(c, cc)
        start(first.at[c], first_t.at[c], mirror, S_MIRROR + c, R_MIRROR + c, on_diagonal)

    own, from_z, from_y, rest = halo(ext_k, 1)
    for cc in range(2):
        arrived(first_t.at[cc], R_MIRROR + cc)
        for c in range(2):
            k = first[c, cc] + first_t[cc, c].T
            if c == cc:
                k += diagonal(c)
            ext_k[cc, 2 * TILE + HALF * c:2 * TILE + HALF * (c + 1), :] = k
        own(cc)
    from_z(0)
    from_z(1)
    from_y(0)
    for cc in range(2):
        if cc:
            from_y(1)
        rest(cc)
        split(ext_k, cc)
        for c in range(2):
            total[cc, c] = 0.25 * first[c, cc] + 0.03125 * product(c, cc)
        start(total.at[cc], total_t.at[cc], mirror, S_MIRROR + 2 + cc, R_MIRROR + 2 + cc, on_diagonal)

    for c in range(2):
        arrived(total_t.at[c], R_MIRROR + 2 + c)
        target = device(2 * core + c, y, z0, zh, x // 2)
        local = jnp.logical_and(mine, part == c)
        for cc in range(2):
            p = ext_p[cc, 2 * TILE + HALF * c:2 * TILE + HALF * (c + 1), :]
            value = p + (total[cc, c] + total_t[c, cc].T)
            if c == cc:
                value += 0.25 * diagonal(c)
            result[c, cc] = value
            start(
                result.at[c, cc],
                o_ref.at[:, pl.ds(pl.multiple_of(TILE * part + HALF * cc, HALF), HALF)],
                target, S_BACK + 2 * c + cc, R_BACK + 2 * part + cc, local,
            )
    for h in range(2):
        for cc in range(2):
            arrived(o_ref.at[:, pl.ds(TILE * h + HALF * cc, HALF)], R_BACK + 2 * h + cc)

    @pl.when(mine)
    def _():
        for t in range(4):
            remote(band.at[0, 0], band.at[0, 0], (row, col), S_BAND + t, 0).wait_send()

    for condition, copy in pending:
        if condition is None:
            copy.wait_send()
        else:
            pl.when(condition)(copy.wait_send)


def body(p_cov, a_blocks, pattern, q_diag):
    base = lax.axis_index("row") * 2
    wanted = (
        base
        + jnp.arange(2, dtype=jnp.int32)[:, None]
        + jnp.arange(WIDTH, dtype=jnp.int32)[None, :]
        - REACH
    )
    hit = pattern[:, None, :] == wanted[:, :, None]
    slots = jnp.max(
        jnp.where(hit, jnp.arange(pattern.shape[1], dtype=jnp.int32)[None, None, :], -1), axis=2
    )
    slots = jnp.where(jnp.logical_and(wanted >= 0, wanted < 64), slots, -1)
    noise = jnp.broadcast_to(q_diag[None, :], (8, HALF))
    vmem = pl.BlockSpec(memory_space=pltpu.VMEM)
    return pl.pallas_call(
        kernel,
        out_shape=jax.ShapeDtypeStruct(p_cov.shape, F32),
        in_specs=[pl.BlockSpec(memory_space=pltpu.SMEM), vmem, vmem, vmem],
        out_specs=vmem,
        scratch_shapes=[
            pltpu.VMEM((2, 2, BS, WIDTH * BS), F32),
            pltpu.VMEM((2, HALF, SPAN), BF16),
            pltpu.VMEM((2, HALF, SPAN), BF16),
            pltpu.VMEM((2, 5 * TILE, HALF), F32),
            pltpu.VMEM((2, 5 * TILE, HALF), F32),
            pltpu.VMEM((2, 5 * TILE, HALF), BF16),
            pltpu.VMEM((2, 5 * TILE, HALF), BF16),
            pltpu.VMEM((2, 2, HALF, HALF), F32),
            pltpu.VMEM((2, 2, HALF, HALF), F32),
            pltpu.VMEM((2, 2, HALF, HALF), F32),
            pltpu.VMEM((2, 2, HALF, HALF), F32),
            pltpu.VMEM((2, 2, HALF, HALF), F32),
            pltpu.VMEM((2, 8, HALF), F32),
            pltpu.SemaphoreType.DMA((N_SEND,)),
            pltpu.SemaphoreType.DMA((N_RECV,)),
        ],
        compiler_params=pltpu.CompilerParams(has_side_effects=True, vmem_limit_bytes=60 * 1024 * 1024),
    )(slots, p_cov, a_blocks, noise)


def solution(mesh):
    return jax.shard_map(
        body,
        mesh=mesh,
        in_specs=(P("row", "col"), P("row", None, None, None), P("row", None), P("row")),
        out_specs=P("row", "col"),
        check_vma=False,
    )
```

```python
import jax
import jax.numpy as jnp
from jax import lax
from jax.experimental import pallas as pl
from jax.experimental.pallas import tpu as pltpu
from jax.sharding import PartitionSpec as P

BS = 128
REACH = 8
WIDTH = 2 * REACH + 1
HALF = 256
QUARTER = 64
TILE = 512
SPAN = (WIDTH + 1) * BS
MESH = pl.DeviceIdType.MESH
F32 = jnp.float32
BF16 = jnp.bfloat16

S_RELAYOUT, S_NOISE, S_BAND, S_FWD, S_HALO, S_MIRROR, S_BACK, N_SEND = 0, 4, 6, 8, 9, 25, 57, 61
R_RELAYOUT, R_NOISE, R_BAND, R_HALO, R_MIRROR, R_BACK, N_RECV = 0, 4, 6, 10, 26, 58, 62


def kernel(
    slot_ref, p_ref, a_ref, q_ref, o_ref,
    strip, band, band_hi, band_lo, ext_p, ext_k, ext_hi, ext_lo,
    first, first_m, first_t, total, total_m, total_t, result, noise, send, recv,
):
    row = lax.axis_index("row")
    col = lax.axis_index("col")
    x, z0, y = row % 4, (row // 4) % 2, row // 8
    core, zh = col % 2, col // 2
    tile_i, tile_j = 4 * y + 2 * z0 + core, 4 * zh + x

    def device(x, y, z0, zh, core):
        return (8 * y + 4 * z0 + x, 2 * zh + core)

    def remote(src, dst, target, s, r):
        return pltpu.make_async_remote_copy(
            src_ref=src, dst_ref=dst, send_sem=send.at[s], recv_sem=recv.at[r],
            device_id=target, device_id_type=MESH,
        )

    pending = []

    def start(src, dst, target, s, r, local=None):
        if local is True:
            pltpu.make_async_copy(src, dst, recv.at[r]).start()
            return
        copy = remote(src, dst, target, s, r)
        if local is None:
            copy.start()
            pending.append((None, copy))
            return
        pl.when(jnp.logical_not(local))(copy.start)
        pl.when(local)(pltpu.make_async_copy(src, dst, recv.at[r]).start)
        pending.append((jnp.logical_not(local), copy))

    def arrived(dst, r):
        remote(dst, dst, (row, col), 0, r).wait_recv()

    partner = device(x, y, z0, zh, 1 - core)

    mine = x // 2 == core
    part = x % 2
    for h in range(2):
        target = device(2 * core + h, y, z0, zh, x // 2)
        local = jnp.logical_and(mine, part == h)
        start(q_ref, noise.at[part], target, S_NOISE + h, R_NOISE + part, local)
    for cc in range(2):
        for h in range(2):
            target = device(2 * core + h, y, z0, zh, x // 2)
            local = jnp.logical_and(mine, part == h)
            start(
                p_ref.at[:, pl.ds(TILE * h + HALF * cc, HALF)],
                ext_p.at[cc, pl.ds(pl.multiple_of(2 * TILE + HALF * part, HALF), HALF), :],
                target, S_RELAYOUT + 2 * cc + h, R_RELAYOUT + 2 * cc + part, local,
            )

    def right(x):
        return (x + 1) % 4

    def left(x):
        return (x + 3) % 4

    def block(b, d):
        slot = slot_ref[b, d]
        return jnp.where(slot >= 0, a_ref[b, jnp.maximum(slot, 0)], 0.0)

    for d in range(WIDTH):
        strip[:, d * BS:(d + 1) * BS] = block(core, d)
    for t, near_x in enumerate((right(x), left(x))):
        start(strip, band.at[part, core], device(near_x, y, z0, zh, x // 2),
              S_BAND + t, R_BAND + 2 * part + core)

    @pl.when(mine)
    def _():
        for b in range(2):
            for d in range(WIDTH):
                band[part, b, :, d * BS:(d + 1) * BS] = block(b, d)

    step = (x + 4 - 2 * core) % 4
    fwd_c = 1 - step % 2
    fwd_right = jnp.logical_or(step == 1, step == 2)
    fwd_b = jnp.where(fwd_right, 0, 1)
    fwd_x = jnp.where(fwd_right, right(x), left(x))

    def forward_band():
        unit = band.at[fwd_c, fwd_b]
        arrived(unit, R_BAND + 2 * fwd_c + fwd_b)
        start(unit, unit, device(fwd_x, y, z0, zh, core), S_FWD, R_BAND + 2 * fwd_c + fwd_b)

    d_slot = jnp.where(z0 == 0, 4, 0)
    y_slot = 4 - d_slot
    y_next = jnp.where(z0 == 0, (y + 1) % 4, (y + 3) % 4)
    near = jnp.where(core == 0, 1, 3)
    f_slot = jnp.where(core == 0, 4, 0)
    f_dst = jnp.where(core == 0, 3, 1)
    f_from_z = f_slot == d_slot

    def halo(ext, base):
        def at(cc, slot):
            return ext.at[cc, pl.ds(pl.multiple_of(slot * TILE, TILE), TILE), :]

        def sem(kind, cc):
            return 8 * base + 2 * kind + cc

        def own(cc):
            start(at(cc, 2), at(cc, y_slot), device(x, y, 1 - z0, zh, core),
                  S_HALO + sem(0, cc), R_HALO + sem(0, cc))
            start(at(cc, 2), at(cc, near), partner, S_HALO + sem(1, cc), R_HALO + sem(1, cc))

        def across(cc):
            start(at(cc, f_slot), at(cc, f_dst), partner,
                  S_HALO + sem(3, cc), R_HALO + sem(3, cc))

        def from_z(cc):
            arrived(at(cc, d_slot), R_HALO + sem(0, cc))
            start(at(cc, d_slot), at(cc, y_slot), device(x, y_next, z0, zh, core),
                  S_HALO + sem(2, cc), R_HALO + sem(2, cc))
            pl.when(f_from_z)(lambda: remote(
                at(cc, f_slot), at(cc, f_dst), partner,
                S_HALO + sem(3, cc), R_HALO + sem(3, cc)).start())

        def from_y(cc):
            arrived(at(cc, y_slot), R_HALO + sem(2, cc))
            pl.when(jnp.logical_not(f_from_z))(lambda: remote(
                at(cc, f_slot), at(cc, f_dst), partner,
                S_HALO + sem(3, cc), R_HALO + sem(3, cc)).start())
            pending.append((None, remote(
                at(cc, f_slot), at(cc, f_dst), partner,
                S_HALO + sem(3, cc), R_HALO + sem(3, cc))))

        def rest(cc):
            arrived(at(cc, 4 - near), R_HALO + sem(1, cc))
            arrived(at(cc, 4 - f_dst), R_HALO + sem(3, cc))

        return own, from_z, from_y, rest

    def split(ext, cc):
        def piece(n, _):
            rows = pl.ds(pl.multiple_of(n * BS, BS), BS)
            value = ext[cc, rows, :]
            hi = value.astype(BF16)
            ext_hi[cc, rows, :] = hi
            ext_lo[cc, rows, :] = (value - hi.astype(F32)).astype(BF16)
            return 0
        lax.fori_loop(0, 5 * TILE // BS, piece, 0)

    def product(c, cc):
        rows = slice(HALF * c, HALF * c + SPAN)
        hi, lo = ext_hi[cc, rows, :], ext_lo[cc, rows, :]
        acc = jnp.dot(band_hi[c], hi, preferred_element_type=F32)
        acc += jnp.dot(band_hi[c], lo, preferred_element_type=F32)
        acc += jnp.dot(band_lo[c], hi, preferred_element_type=F32)
        return acc

    def split_band(c):
        for b in range(2):
            empty = slice(0, BS) if b else slice(WIDTH * BS, SPAN)
            rows = slice(b * BS, (b + 1) * BS)
            band_hi[c, rows, empty] = jnp.zeros((BS, BS), BF16)
            band_lo[c, rows, empty] = jnp.zeros((BS, BS), BF16)
            for d in range(WIDTH):
                value = band[c, b, :, d * BS:(d + 1) * BS]
                hi = value.astype(BF16)
                cols = slice((b + d) * BS, (b + d + 1) * BS)
                band_hi[c, rows, cols] = hi
                band_lo[c, rows, cols] = (value - hi.astype(F32)).astype(BF16)

    def mirror(base, src, mid, dst):
        def quarter(ref, c, n):
            return ref.at[c, :, pl.ds(pl.multiple_of(n * QUARTER, QUARTER), QUARTER), :]

        def spread(c):
            for n in (1, 3, 2, 0):
                r = (y + n) % 4
                start(quarter(src, c, r), quarter(mid, c, y), device(x, r, z0, zh, core),
                      S_MIRROR + 16 * base + 8 * c + n, R_MIRROR + 16 * base + 8 * c + y,
                      None if n else True)

        def onward(c):
            for n in (0, 1, 3, 2):
                r = (y + n) % 4
                unit = quarter(mid, c, r)
                arrived(unit, R_MIRROR + 16 * base + 8 * c + r)
                here = (x == 2 * z0 + core) & (y == zh) & (z0 == x // 2) & (zh == r) & (core == x % 2)
                start(unit, quarter(dst, c, y), device(2 * z0 + core, zh, x // 2, r, x % 2),
                      S_MIRROR + 16 * base + 8 * c + 4 + n, R_MIRROR + 16 * base + 8 * c + 4 + y,
                      here)

        def landed(c):
            for r in range(4):
                arrived(quarter(dst, c, r), R_MIRROR + 16 * base + 8 * c + 4 + r)

        return spread, onward, landed

    on_diagonal = tile_i == tile_j
    eye = (
        lax.broadcasted_iota(jnp.int32, (HALF, HALF), 0)
        == lax.broadcasted_iota(jnp.int32, (HALF, HALF), 1)
    )

    def diagonal(c):
        values = jnp.broadcast_to(noise[c, 0:1, :], (HALF, HALF))
        return jnp.where(jnp.logical_and(eye, on_diagonal), values, 0.0)

    own, from_z, from_y, rest = halo(ext_p, 0)
    for cc in range(2):
        for c in range(2):
            arrived(ext_p.at[cc, pl.ds(2 * TILE + HALF * c, HALF), :], R_RELAYOUT + 2 * cc + c)
        own(cc)
    from_z(0)
    from_z(1)
    from_y(0)
    from_y(1)
    forward_band()
    for cc in range(2):
        rest(cc)
        split(ext_p, cc)
    for c in range(2):
        arrived(noise.at[c], R_NOISE + c)

    spread, onward, landed = mirror(0, first, first_m, first_t)
    for c in range(2):
        for b in range(2):
            seen = jnp.logical_and(fwd_c == c, fwd_b == b)
            held = jnp.logical_and(mine, part == c)
            skip = jnp.logical_or(seen, held)
            pl.when(jnp.logical_not(skip))(
                lambda c=c, b=b: arrived(band.at[c, b], R_BAND + 2 * c + b))
        split_band(c)
        for cc in range(2):
            first[c, cc] = product(c, cc)
        spread(c)
    onward(0)
    onward(1)

    own, from_z, from_y, rest = halo(ext_k, 1)
    for cc in range(2):
        landed(cc)
        for c in range(2):
            k = first[c, cc] + first_t[cc, c].T
            if c == cc:
                k += diagonal(c)
            ext_k[cc, 2 * TILE + HALF * c:2 * TILE + HALF * (c + 1), :] = k
        own(cc)
    from_z(0)
    from_z(1)
    from_y(0)
    spread, onward, landed = mirror(1, total, total_m, total_t)
    for cc in range(2):
        rest(cc)
        split(ext_k, cc)
        for c in range(2):
            total[cc, c] = 0.25 * first[c, cc] + 0.03125 * product(c, cc)
        spread(cc)
        if cc == 0:
            from_y(1)
        onward(cc)

    for c in range(2):
        landed(c)
        target = device(2 * core + c, y, z0, zh, x // 2)
        local = jnp.logical_and(mine, part == c)
        for cc in range(2):
            p = ext_p[cc, 2 * TILE + HALF * c:2 * TILE + HALF * (c + 1), :]
            value = p + (total[cc, c] + total_t[c, cc].T)
            if c == cc:
                value += 0.25 * diagonal(c)
            result[c, cc] = value
            start(
                result.at[c, cc],
                o_ref.at[:, pl.ds(pl.multiple_of(TILE * part + HALF * cc, HALF), HALF)],
                target, S_BACK + 2 * c + cc, R_BACK + 2 * part + cc, local,
            )
    for h in range(2):
        for cc in range(2):
            arrived(o_ref.at[:, pl.ds(TILE * h + HALF * cc, HALF)], R_BACK + 2 * h + cc)

    for condition, copy in pending:
        if condition is None:
            copy.wait_send()
        else:
            pl.when(condition)(copy.wait_send)


def body(p_cov, a_blocks, pattern, q_diag):
    base = lax.axis_index("row") * 2
    wanted = (
        base
        + jnp.arange(2, dtype=jnp.int32)[:, None]
        + jnp.arange(WIDTH, dtype=jnp.int32)[None, :]
        - REACH
    )
    hit = pattern[:, None, :] == wanted[:, :, None]
    slots = jnp.max(
        jnp.where(hit, jnp.arange(pattern.shape[1], dtype=jnp.int32)[None, None, :], -1), axis=2
    )
    slots = jnp.where(jnp.logical_and(wanted >= 0, wanted < 64), slots, -1)
    noise = jnp.broadcast_to(q_diag[None, :], (8, HALF))
    vmem = pl.BlockSpec(memory_space=pltpu.VMEM)
    return pl.pallas_call(
        kernel,
        out_shape=jax.ShapeDtypeStruct(p_cov.shape, F32),
        in_specs=[pl.BlockSpec(memory_space=pltpu.SMEM), vmem, vmem, vmem],
        out_specs=vmem,
        scratch_shapes=[
            pltpu.VMEM((BS, WIDTH * BS), F32),
            pltpu.VMEM((2, 2, BS, WIDTH * BS), F32),
            pltpu.VMEM((2, HALF, SPAN), BF16),
            pltpu.VMEM((2, HALF, SPAN), BF16),
            pltpu.VMEM((2, 5 * TILE, HALF), F32),
            pltpu.VMEM((2, 5 * TILE, HALF), F32),
            pltpu.VMEM((2, 5 * TILE, HALF), BF16),
            pltpu.VMEM((2, 5 * TILE, HALF), BF16),
            *[pltpu.VMEM((2, 2, HALF, HALF), F32)] * 7,
            pltpu.VMEM((2, 8, HALF), F32),
            pltpu.SemaphoreType.DMA((N_SEND,)),
            pltpu.SemaphoreType.DMA((N_RECV,)),
        ],
        compiler_params=pltpu.CompilerParams(has_side_effects=True, vmem_limit_bytes=60 * 1024 * 1024),
    )(slots, p_cov, a_blocks, noise)


def solution(mesh):
    return jax.shard_map(
        body,
        mesh=mesh,
        in_specs=(P("row", "col"), P("row", None, None, None), P("row", None), P("row")),
        out_specs=P("row", "col"),
        check_vma=False,
    )
```

```python
import jax
import jax.numpy as jnp
from jax import lax
from jax.experimental import pallas as pl
from jax.experimental.pallas import tpu as pltpu
from jax.sharding import PartitionSpec as P

BS = 128
REACH = 8
WIDTH = 2 * REACH + 1
HALF = 256
QUARTER = 64
TILE = 512
SPAN = (WIDTH + 1) * BS
MESH = pl.DeviceIdType.MESH
F32 = jnp.float32
BF16 = jnp.bfloat16

S_RELAYOUT, S_NOISE, S_BAND, S_FWD, S_HALO, S_MIRROR, S_BACK, N_SEND = 0, 4, 6, 8, 9, 41, 105, 109
R_RELAYOUT, R_NOISE, R_BAND, R_HALO, R_MIRROR, R_BACK, N_RECV = 0, 4, 6, 10, 42, 106, 110


def kernel(
    pattern_ref, p_ref, a_hbm, q_ref, o_ref,
    a_ref, own_noise, strip, band, band_hi, band_lo, ext_p, ext_k, ext_hi, ext_lo,
    first, first_m, first_t, total, total_m, total_t, result, noise, send, recv, load,
):
    row = lax.axis_index("row")
    col = lax.axis_index("col")
    x, z0, y = row % 4, (row // 4) % 2, row // 8
    core, zh = col % 2, col // 2
    tile_i, tile_j = 4 * y + 2 * z0 + core, 4 * zh + 2 * (x % 2) + x // 2

    def device(x, y, z0, zh, core):
        return (8 * y + 4 * z0 + x, 2 * zh + core)

    def remote(src, dst, target, s, r):
        return pltpu.make_async_remote_copy(
            src_ref=src, dst_ref=dst, send_sem=send.at[s], recv_sem=recv.at[r],
            device_id=target, device_id_type=MESH,
        )

    pending = []

    def start(src, dst, target, s, r, local=None):
        if local is True:
            pltpu.make_async_copy(src, dst, recv.at[r]).start()
            return
        copy = remote(src, dst, target, s, r)
        if local is None:
            copy.start()
            pending.append((None, copy))
            return
        pl.when(jnp.logical_not(local))(copy.start)
        pl.when(local)(pltpu.make_async_copy(src, dst, recv.at[r]).start)
        pending.append((jnp.logical_not(local), copy))

    def arrived(dst, r):
        remote(dst, dst, (row, col), 0, r).wait_recv()

    partner = device(x, y, z0, zh, 1 - core)

    a_load = pltpu.make_async_copy(a_hbm, a_ref, load)
    a_load.start()
    own_noise[...] = jnp.broadcast_to(q_ref[...], own_noise.shape)

    mine = x // 2 == core
    part = x % 2

    def strip_target(h):
        return device(core + 2 * h, y, z0, zh, x // 2), mine & (core + 2 * h == x)

    for cc in range(2):
        for h in range(2):
            target, local = strip_target(h)
            start(
                p_ref.at[:, pl.ds(TILE * h + HALF * cc, HALF)],
                ext_p.at[cc, pl.ds(pl.multiple_of(2 * TILE + HALF * part, HALF), HALF), :],
                target, S_RELAYOUT + 2 * cc + h, R_RELAYOUT + 2 * cc + part, local,
            )

    for h in range(2):
        target, local = strip_target(h)
        start(own_noise, noise.at[part], target, S_NOISE + h, R_NOISE + part, local)

    def right(x):
        return (x + 1) % 4

    def left(x):
        return (x + 3) % 4

    def split_band(c):
        for b in range(2):
            empty = slice(0, BS) if b else slice(WIDTH * BS, SPAN)
            rows = slice(b * BS, (b + 1) * BS)
            band_hi[c, rows, empty] = jnp.zeros((BS, BS), BF16)
            band_lo[c, rows, empty] = jnp.zeros((BS, BS), BF16)
            for d in range(WIDTH):
                value = band[c, b, :, d * BS:(d + 1) * BS]
                hi = value.astype(BF16)
                cols = slice((b + d) * BS, (b + d + 1) * BS)
                band_hi[c, rows, cols] = hi
                band_lo[c, rows, cols] = (value - hi.astype(F32)).astype(BF16)

    def block(b, d):
        wanted, slot = 2 * row + b + d - REACH, -1
        for s in range(pattern_ref.shape[1]):
            slot = jnp.where(pattern_ref[b, s] == wanted, s, slot)
        slot = jnp.where(wanted >= 0, slot, -1)
        return jnp.where(slot >= 0, a_ref[b, jnp.maximum(slot, 0)], 0.0)

    a_load.wait()
    for d in range(WIDTH):
        strip[:, d * BS:(d + 1) * BS] = block(core, d)
    for t, near_x in enumerate((right(x), left(x))):
        start(strip, band.at[part, core], device(near_x, y, z0, zh, x // 2),
              S_BAND + t, R_BAND + 2 * part + core)

    @pl.when(mine)
    def _():
        for b in range(2):
            for d in range(WIDTH):
                band[part, b, :, d * BS:(d + 1) * BS] = block(b, d)
        split_band(part)

    step = (x + 4 - 2 * core) % 4
    fwd_c = 1 - step % 2
    fwd_right = jnp.logical_or(step == 1, step == 2)
    fwd_b = jnp.where(fwd_right, 0, 1)
    fwd_x = jnp.where(fwd_right, right(x), left(x))

    def forward_band():
        unit = band.at[fwd_c, fwd_b]
        arrived(unit, R_BAND + 2 * fwd_c + fwd_b)
        fwd_copy.start()

    fwd_copy = remote(band.at[fwd_c, fwd_b], band.at[fwd_c, fwd_b],
                      device(fwd_x, y, z0, zh, core), S_FWD, R_BAND + 2 * fwd_c + fwd_b)
    pending.append((None, fwd_copy))

    d_slot = jnp.where(z0 == 0, 4, 0)
    y_slot = 4 - d_slot
    y_next = jnp.where(z0 == 0, (y + 1) % 4, (y + 3) % 4)
    near = jnp.where(core == 0, 1, 3)
    f_slot = jnp.where(core == 0, 4, 0)
    f_dst = jnp.where(core == 0, 3, 1)
    f_from_z = f_slot == d_slot

    def halo(ext, base):
        def at(v, slot):
            return ext.at[v // 2, pl.ds(pl.multiple_of(slot * TILE + HALF * (v % 2), HALF), HALF), :]

        def sem(kind, v):
            return 16 * base + 4 * kind + v

        def own(v):
            start(at(v, 2), at(v, y_slot), device(x, y, 1 - z0, zh, core),
                  S_HALO + sem(0, v), R_HALO + sem(0, v))
            start(at(v, 2), at(v, near), partner, S_HALO + sem(1, v), R_HALO + sem(1, v))

        def across(v):
            return remote(at(v, f_slot), at(v, f_dst), partner,
                          S_HALO + sem(3, v), R_HALO + sem(3, v))

        def from_z(v):
            arrived(at(v, d_slot), R_HALO + sem(0, v))
            start(at(v, d_slot), at(v, y_slot), device(x, y_next, z0, zh, core),
                  S_HALO + sem(2, v), R_HALO + sem(2, v))
            pl.when(f_from_z)(lambda: across(v).start())

        def from_y(v):
            arrived(at(v, y_slot), R_HALO + sem(2, v))
            pl.when(jnp.logical_not(f_from_z))(lambda: across(v).start())
            pending.append((None, across(v)))

        def rest(v):
            arrived(at(v, 4 - near), R_HALO + sem(1, v))
            arrived(at(v, 4 - f_dst), R_HALO + sem(3, v))

        return own, from_z, from_y, rest

    def split(ext, cc):
        def piece(n, _):
            rows = pl.ds(pl.multiple_of(n * BS, BS), BS)
            value = ext[cc, rows, :]
            hi = value.astype(BF16)
            ext_hi[cc, rows, :] = hi
            ext_lo[cc, rows, :] = (value - hi.astype(F32)).astype(BF16)
            return 0
        lax.fori_loop(0, 5 * TILE // BS, piece, 0)

    def product(c, cc):
        rows = pl.ds(pl.multiple_of(HALF * c, HALF), SPAN)
        hi, lo = ext_hi[cc, rows, :], ext_lo[cc, rows, :]
        acc = jnp.dot(band_hi[c], hi, preferred_element_type=F32)
        acc += jnp.dot(band_hi[c], lo, preferred_element_type=F32)
        acc += jnp.dot(band_lo[c], hi, preferred_element_type=F32)
        return acc

    def mirror(base, src, mid, dst):
        def quarter(ref, c, d, n):
            return ref.at[c, d, pl.ds(pl.multiple_of(n * QUARTER, QUARTER), QUARTER), :]

        def spread(c, d):
            base_s, base_r = S_MIRROR + 32 * base + 16 * c + 8 * d, R_MIRROR + 32 * base + 16 * c + 8 * d
            for n in (1, 3, 2, 0):
                r = (y + n) % 4
                start(quarter(src, c, d, r), quarter(mid, c, d, y), device(x, r, z0, zh, core),
                      base_s + n, base_r + y, None if n else True)

        def onward(c, d):
            base_s, base_r = S_MIRROR + 32 * base + 16 * c + 8 * d, R_MIRROR + 32 * base + 16 * c + 8 * d
            for n in (0, 1, 3, 2):
                r = (y + n) % 4
                unit = quarter(mid, c, d, r)
                arrived(unit, base_r + r)
                here = (x == z0 + 2 * core) & (y == zh) & (z0 == part) & (zh == r) & mine
                start(unit, quarter(dst, c, d, y), device(z0 + 2 * core, zh, part, r, x // 2),
                      base_s + 4 + n, base_r + 4 + y, here)

        def landed(c, d):
            for r in range(4):
                arrived(quarter(dst, c, d, r), R_MIRROR + 32 * base + 16 * c + 8 * d + 4 + r)

        return spread, onward, landed

    on_diagonal = tile_i == tile_j
    eye = (
        lax.broadcasted_iota(jnp.int32, (HALF, HALF), 0)
        == lax.broadcasted_iota(jnp.int32, (HALF, HALF), 1)
    )

    def diagonal(c):
        values = jnp.broadcast_to(noise[c, 0:1, :], (HALF, HALF))
        return jnp.where(jnp.logical_and(eye, on_diagonal), values, 0.0)

    own, from_z, from_y, rest = halo(ext_p, 0)
    for v in range(4):
        arrived(ext_p.at[v // 2, pl.ds(2 * TILE + HALF * (v % 2), HALF), :], R_RELAYOUT + v)
        own(v)
    for n in range(5):
        if n < 4:
            from_z(n)
        if n > 0:
            from_y(n - 1)
    for cc in range(2):
        rest(2 * cc)
        rest(2 * cc + 1)
        split(ext_p, cc)
    for c in range(2):
        arrived(noise.at[c], R_NOISE + c)

    spread, onward, landed = mirror(0, first, first_m, first_t)
    other = jnp.logical_not(mine)
    soon = jnp.where((step == 1) | (step == 2), 1, 0)
    late = 1 - soon

    @pl.when(other)
    def _():
        forward_band()
        arrived(band.at[soon, 1 - fwd_b], R_BAND + 2 * soon + 1 - fwd_b)
        split_band(soon)

    for cc in range(2):
        first[soon, cc] = product(soon, cc)
        spread(soon, cc)
    pl.when(mine)(forward_band)
    onward(soon, 0)
    onward(soon, 1)
    pl.when(other)(lambda: arrived(band.at[late, fwd_b], R_BAND + 2 * late + fwd_b))
    arrived(band.at[late, 1 - fwd_b], R_BAND + 2 * late + 1 - fwd_b)
    split_band(late)
    for cc in range(2):
        first[late, cc] = product(late, cc)
        spread(late, cc)
    onward(late, 0)
    onward(late, 1)

    own, from_z, from_y, rest = halo(ext_k, 1)

    def combine(cc):
        for c in range(2):
            landed(cc, c)
            k = first[c, cc] + first_t[cc, c].T
            if c == cc:
                k += diagonal(c)
            ext_k[cc, 2 * TILE + HALF * c:2 * TILE + HALF * (c + 1), :] = k
            own(2 * cc + c)

    spread, onward, landed_total = mirror(1, total, total_m, total_t)

    def apply(cc):
        rest(2 * cc)
        rest(2 * cc + 1)
        split(ext_k, cc)
        for c in range(2):
            total[cc, c] = 0.25 * first[c, cc] + 0.03125 * product(c, cc)
            spread(cc, c)

    combine(0)
    from_z(0)
    from_z(1)
    combine(1)
    from_y(0)
    from_z(2)
    from_y(1)
    from_z(3)
    apply(0)
    from_y(2)
    from_y(3)
    onward(0, 0)
    onward(0, 1)
    apply(1)
    onward(1, 0)
    onward(1, 1)

    for c in range(2):
        target = device(2 * core + c, y, z0, zh, part)
        local = (2 * core + c == x) & (part == core)
        for cc in range(2):
            landed_total(c, cc)
            p = ext_p[cc, 2 * TILE + HALF * c:2 * TILE + HALF * (c + 1), :]
            value = p + (total[cc, c] + total_t[c, cc].T)
            if c == cc:
                value += 0.25 * diagonal(c)
            result[c, cc] = value
            start(
                result.at[c, cc],
                o_ref.at[:, pl.ds(pl.multiple_of(TILE * (x // 2) + HALF * cc, HALF), HALF)],
                target, S_BACK + 2 * c + cc, R_BACK + 2 * (x // 2) + cc, local,
            )
    for h in range(2):
        for cc in range(2):
            arrived(o_ref.at[:, pl.ds(TILE * h + HALF * cc, HALF)], R_BACK + 2 * h + cc)

    for condition, copy in pending:
        if condition is None:
            copy.wait_send()
        else:
            pl.when(condition)(copy.wait_send)


def body(p_cov, a_blocks, pattern, q_diag):
    vmem = pl.BlockSpec(memory_space=pltpu.VMEM)
    return pl.pallas_call(
        kernel,
        out_shape=jax.ShapeDtypeStruct(p_cov.shape, F32),
        in_specs=[
            pl.BlockSpec(memory_space=pltpu.SMEM),
            pl.BlockSpec(memory_space=pl.ANY),
            pl.BlockSpec(memory_space=pl.ANY),
            vmem,
        ],
        out_specs=vmem,
        scratch_shapes=[
            pltpu.VMEM(a_blocks.shape, F32),
            pltpu.VMEM((8, HALF), F32),
            pltpu.VMEM((BS, WIDTH * BS), F32),
            pltpu.VMEM((2, 2, BS, WIDTH * BS), F32),
            pltpu.VMEM((2, HALF, SPAN), BF16),
            pltpu.VMEM((2, HALF, SPAN), BF16),
            pltpu.VMEM((2, 5 * TILE, HALF), F32),
            pltpu.VMEM((2, 5 * TILE, HALF), F32),
            pltpu.VMEM((2, 5 * TILE, HALF), BF16),
            pltpu.VMEM((2, 5 * TILE, HALF), BF16),
            *[pltpu.VMEM((2, 2, HALF, HALF), F32)] * 7,
            pltpu.VMEM((2, 8, HALF), F32),
            pltpu.SemaphoreType.DMA((N_SEND,)),
            pltpu.SemaphoreType.DMA((N_RECV,)),
            pltpu.SemaphoreType.DMA(()),
        ],
        compiler_params=pltpu.CompilerParams(has_side_effects=True, vmem_limit_bytes=60 * 1024 * 1024),
    )(pattern, p_cov, a_blocks, q_diag.reshape(1, HALF))


def solution(mesh):
    return jax.shard_map(
        body,
        mesh=mesh,
        in_specs=(P("row", "col"), P("row", None, None, None), P("row", None), P("row")),
        out_specs=P("row", "col"),
        check_vma=False,
    )
```

```python
import jax
import jax.numpy as jnp
from jax import lax
from jax.experimental import pallas as pl
from jax.experimental.pallas import tpu as pltpu
from jax.sharding import PartitionSpec as P

BS = 128
REACH = 8
WIDTH = 2 * REACH + 1
HALF = 256
QUARTER = 64
TILE = 512
SPAN = (WIDTH + 1) * BS
MESH = pl.DeviceIdType.MESH
F32 = jnp.float32
BF16 = jnp.bfloat16

S_RELAYOUT, S_NOISE, S_BAND, S_FWD, S_HALO, S_MIRROR, S_BACK, N_SEND = 0, 4, 6, 8, 9, 41, 105, 109
R_RELAYOUT, R_NOISE, R_BAND, R_HALO, R_MIRROR, R_BACK, N_RECV = 0, 4, 6, 10, 42, 106, 110


def kernel(
    pattern_ref, p_ref, a_hbm, q_ref, o_ref,
    a_ref, own_noise, strip, band, band_hi, band_lo, ext_p, ext_k, ext_hi, ext_lo,
    first, first_m, first_t, total, total_m, total_t, result, noise, send, recv, load,
):
    row = lax.axis_index("row")
    col = lax.axis_index("col")
    x, z0, y = row % 4, (row // 4) % 2, row // 8
    core, zh = col % 2, col // 2
    j1 = (x + zh) % 2
    tile_i, tile_j = 4 * y + 2 * z0 + core, 4 * zh + 2 * j1 + x // 2

    def device(x, y, z0, zh, core):
        return (8 * y + 4 * z0 + x, 2 * zh + core)

    def remote(src, dst, target, s, r):
        return pltpu.make_async_remote_copy(
            src_ref=src, dst_ref=dst, send_sem=send.at[s], recv_sem=recv.at[r],
            device_id=target, device_id_type=MESH,
        )

    pending = []

    def start(src, dst, target, s, r, local=None):
        if local is True:
            pltpu.make_async_copy(src, dst, recv.at[r]).start()
            return
        copy = remote(src, dst, target, s, r)
        if local is None:
            copy.start()
            pending.append((None, copy))
            return
        pl.when(jnp.logical_not(local))(copy.start)
        pl.when(local)(pltpu.make_async_copy(src, dst, recv.at[r]).start)
        pending.append((jnp.logical_not(local), copy))

    def arrived(dst, r):
        remote(dst, dst, (row, col), 0, r).wait_recv()

    partner = device(x, y, z0, zh, 1 - core)

    a_load = pltpu.make_async_copy(a_hbm, a_ref, load)
    a_load.start()
    own_noise[...] = jnp.broadcast_to(q_ref[...], own_noise.shape)

    mine = x // 2 == core
    part = x % 2

    def strip_target(h):
        x_to = (core + zh) % 2 + 2 * h
        return device(x_to, y, z0, zh, x // 2), mine & (x_to == x)

    for cc in range(2):
        for h in range(2):
            target, local = strip_target(h)
            start(
                p_ref.at[:, pl.ds(TILE * h + HALF * cc, HALF)],
                ext_p.at[cc, pl.ds(pl.multiple_of(2 * TILE + HALF * part, HALF), HALF), :],
                target, S_RELAYOUT + 2 * cc + h, R_RELAYOUT + 2 * cc + part, local,
            )

    for h in range(2):
        target, local = strip_target(h)
        start(own_noise, noise.at[part], target, S_NOISE + h, R_NOISE + part, local)

    def right(x):
        return (x + 1) % 4

    def left(x):
        return (x + 3) % 4

    def split_band(c):
        for b in range(2):
            empty = slice(0, BS) if b else slice(WIDTH * BS, SPAN)
            rows = slice(b * BS, (b + 1) * BS)
            band_hi[c, rows, empty] = jnp.zeros((BS, BS), BF16)
            band_lo[c, rows, empty] = jnp.zeros((BS, BS), BF16)
            for d in range(WIDTH):
                value = band[c, b, :, d * BS:(d + 1) * BS]
                hi = value.astype(BF16)
                cols = slice((b + d) * BS, (b + d + 1) * BS)
                band_hi[c, rows, cols] = hi
                band_lo[c, rows, cols] = (value - hi.astype(F32)).astype(BF16)

    def block(b, d):
        wanted, slot = 2 * row + b + d - REACH, -1
        for s in range(pattern_ref.shape[1]):
            slot = jnp.where(pattern_ref[b, s] == wanted, s, slot)
        slot = jnp.where(wanted >= 0, slot, -1)
        return jnp.where(slot >= 0, a_ref[b, jnp.maximum(slot, 0)], 0.0)

    a_load.wait()
    for d in range(WIDTH):
        strip[:, d * BS:(d + 1) * BS] = block(core, d)
    for t, near_x in enumerate((right(x), left(x))):
        start(strip, band.at[part, core], device(near_x, y, z0, zh, x // 2),
              S_BAND + t, R_BAND + 2 * part + core)

    @pl.when(mine)
    def _():
        for b in range(2):
            for d in range(WIDTH):
                band[part, b, :, d * BS:(d + 1) * BS] = block(b, d)
        split_band(part)

    step = (x + 4 - 2 * core) % 4
    fwd_c = 1 - step % 2
    fwd_right = jnp.logical_or(step == 1, step == 2)
    fwd_b = jnp.where(fwd_right, 0, 1)
    fwd_x = jnp.where(fwd_right, right(x), left(x))

    def forward_band():
        unit = band.at[fwd_c, fwd_b]
        arrived(unit, R_BAND + 2 * fwd_c + fwd_b)
        fwd_copy.start()

    fwd_copy = remote(band.at[fwd_c, fwd_b], band.at[fwd_c, fwd_b],
                      device(fwd_x, y, z0, zh, core), S_FWD, R_BAND + 2 * fwd_c + fwd_b)
    pending.append((None, fwd_copy))

    d_slot = jnp.where(z0 == 0, 4, 0)
    y_slot = 4 - d_slot
    y_next = jnp.where(z0 == 0, (y + 1) % 4, (y + 3) % 4)
    near = jnp.where(core == 0, 1, 3)
    f_slot = jnp.where(core == 0, 4, 0)
    f_dst = jnp.where(core == 0, 3, 1)
    f_from_z = f_slot == d_slot

    def halo(ext, base):
        def at(v, slot):
            return ext.at[v // 2, pl.ds(pl.multiple_of(slot * TILE + HALF * (v % 2), HALF), HALF), :]

        def sem(kind, v):
            return 16 * base + 4 * kind + v

        def own(v):
            start(at(v, 2), at(v, y_slot), device(x, y, 1 - z0, zh, core),
                  S_HALO + sem(0, v), R_HALO + sem(0, v))
            start(at(v, 2), at(v, near), partner, S_HALO + sem(1, v), R_HALO + sem(1, v))

        def across(v):
            return remote(at(v, f_slot), at(v, f_dst), partner,
                          S_HALO + sem(3, v), R_HALO + sem(3, v))

        def from_z(v):
            arrived(at(v, d_slot), R_HALO + sem(0, v))
            start(at(v, d_slot), at(v, y_slot), device(x, y_next, z0, zh, core),
                  S_HALO + sem(2, v), R_HALO + sem(2, v))
            pl.when(f_from_z)(lambda: across(v).start())

        def from_y(v):
            arrived(at(v, y_slot), R_HALO + sem(2, v))
            pl.when(jnp.logical_not(f_from_z))(lambda: across(v).start())
            pending.append((None, across(v)))

        def rest(v):
            arrived(at(v, 4 - near), R_HALO + sem(1, v))
            arrived(at(v, 4 - f_dst), R_HALO + sem(3, v))

        return own, from_z, from_y, rest

    def split(ext, cc):
        def piece(n, _):
            rows = pl.ds(pl.multiple_of(n * BS, BS), BS)
            value = ext[cc, rows, :]
            hi = value.astype(BF16)
            ext_hi[cc, rows, :] = hi
            ext_lo[cc, rows, :] = (value - hi.astype(F32)).astype(BF16)
            return 0
        lax.fori_loop(0, 5 * TILE // BS, piece, 0)

    def product(c, cc):
        rows = pl.ds(pl.multiple_of(HALF * c, HALF), SPAN)
        hi, lo = ext_hi[cc, rows, :], ext_lo[cc, rows, :]
        acc = jnp.dot(band_hi[c], hi, preferred_element_type=F32)
        acc += jnp.dot(band_hi[c], lo, preferred_element_type=F32)
        acc += jnp.dot(band_lo[c], hi, preferred_element_type=F32)
        return acc

    def mirror(base, src, mid, dst):
        def quarter(ref, c, d, n):
            return ref.at[c, d, pl.ds(pl.multiple_of(n * QUARTER, QUARTER), QUARTER), :]

        def spread(c, d):
            base_s, base_r = S_MIRROR + 32 * base + 16 * c + 8 * d, R_MIRROR + 32 * base + 16 * c + 8 * d
            for n in (1, 3, 2, 0):
                r = (y + n) % 4
                start(quarter(src, c, d, r), quarter(mid, c, d, y), device(x, r, z0, zh, core),
                      base_s + n, base_r + y, None if n else True)

        def onward(c, d):
            base_s, base_r = S_MIRROR + 32 * base + 16 * c + 8 * d, R_MIRROR + 32 * base + 16 * c + 8 * d
            for n in (0, 1, 3, 2):
                r = (y + n) % 4
                unit = quarter(mid, c, d, r)
                arrived(unit, base_r + r)
                x_to = (z0 + r) % 2 + 2 * core
                here = (x == x_to) & (y == zh) & (z0 == j1) & (zh == r) & mine
                start(unit, quarter(dst, c, d, y), device(x_to, zh, j1, r, x // 2),
                      base_s + 4 + n, base_r + 4 + y, here)

        def landed(c, d):
            for r in range(4):
                arrived(quarter(dst, c, d, r), R_MIRROR + 32 * base + 16 * c + 8 * d + 4 + r)

        return spread, onward, landed

    on_diagonal = tile_i == tile_j
    eye = (
        lax.broadcasted_iota(jnp.int32, (HALF, HALF), 0)
        == lax.broadcasted_iota(jnp.int32, (HALF, HALF), 1)
    )

    def diagonal(c):
        values = jnp.broadcast_to(noise[c, 0:1, :], (HALF, HALF))
        return jnp.where(jnp.logical_and(eye, on_diagonal), values, 0.0)

    own, from_z, from_y, rest = halo(ext_p, 0)
    for v in range(4):
        arrived(ext_p.at[v // 2, pl.ds(2 * TILE + HALF * (v % 2), HALF), :], R_RELAYOUT + v)
        own(v)
    for n in range(5):
        if n < 4:
            from_z(n)
        if n > 0:
            from_y(n - 1)
    for cc in range(2):
        rest(2 * cc)
        rest(2 * cc + 1)
        split(ext_p, cc)
    for c in range(2):
        arrived(noise.at[c], R_NOISE + c)

    spread, onward, landed = mirror(0, first, first_m, first_t)
    other = jnp.logical_not(mine)
    soon = jnp.where((step == 1) | (step == 2), 1, 0)
    late = 1 - soon

    @pl.when(other)
    def _():
        forward_band()
        arrived(band.at[soon, 1 - fwd_b], R_BAND + 2 * soon + 1 - fwd_b)
        split_band(soon)

    for cc in range(2):
        first[soon, cc] = product(soon, cc)
        spread(soon, cc)
    pl.when(mine)(forward_band)
    onward(soon, 0)
    onward(soon, 1)
    pl.when(other)(lambda: arrived(band.at[late, fwd_b], R_BAND + 2 * late + fwd_b))
    arrived(band.at[late, 1 - fwd_b], R_BAND + 2 * late + 1 - fwd_b)
    split_band(late)
    for cc in range(2):
        first[late, cc] = product(late, cc)
        spread(late, cc)
    onward(late, 0)
    onward(late, 1)

    own, from_z, from_y, rest = halo(ext_k, 1)

    def combine(cc):
        for c in range(2):
            landed(cc, c)
            k = first[c, cc] + first_t[cc, c].T
            if c == cc:
                k += diagonal(c)
            ext_k[cc, 2 * TILE + HALF * c:2 * TILE + HALF * (c + 1), :] = k
            own(2 * cc + c)

    spread, onward, landed_total = mirror(1, total, total_m, total_t)

    def apply(cc):
        rest(2 * cc)
        rest(2 * cc + 1)
        split(ext_k, cc)
        for c in range(2):
            total[cc, c] = 0.25 * first[c, cc] + 0.03125 * product(c, cc)
            spread(cc, c)

    combine(0)
    from_z(0)
    from_z(1)
    combine(1)
    from_y(0)
    from_z(2)
    from_y(1)
    from_z(3)
    apply(0)
    from_y(2)
    from_y(3)
    onward(0, 0)
    onward(0, 1)
    apply(1)
    onward(1, 0)
    onward(1, 1)

    for c in range(2):
        target = device(2 * core + c, y, z0, zh, j1)
        local = (2 * core + c == x) & (j1 == core)
        for cc in range(2):
            landed_total(c, cc)
            p = ext_p[cc, 2 * TILE + HALF * c:2 * TILE + HALF * (c + 1), :]
            value = p + (total[cc, c] + total_t[c, cc].T)
            if c == cc:
                value += 0.25 * diagonal(c)
            result[c, cc] = value
            start(
                result.at[c, cc],
                o_ref.at[:, pl.ds(pl.multiple_of(TILE * (x // 2) + HALF * cc, HALF), HALF)],
                target, S_BACK + 2 * c + cc, R_BACK + 2 * (x // 2) + cc, local,
            )
    for h in range(2):
        for cc in range(2):
            arrived(o_ref.at[:, pl.ds(TILE * h + HALF * cc, HALF)], R_BACK + 2 * h + cc)

    for condition, copy in pending:
        if condition is None:
            copy.wait_send()
        else:
            pl.when(condition)(copy.wait_send)


def body(p_cov, a_blocks, pattern, q_diag):
    vmem = pl.BlockSpec(memory_space=pltpu.VMEM)
    return pl.pallas_call(
        kernel,
        out_shape=jax.ShapeDtypeStruct(p_cov.shape, F32),
        in_specs=[
            pl.BlockSpec(memory_space=pltpu.SMEM),
            pl.BlockSpec(memory_space=pl.ANY),
            pl.BlockSpec(memory_space=pl.ANY),
            vmem,
        ],
        out_specs=vmem,
        scratch_shapes=[
            pltpu.VMEM(a_blocks.shape, F32),
            pltpu.VMEM((8, HALF), F32),
            pltpu.VMEM((BS, WIDTH * BS), F32),
            pltpu.VMEM((2, 2, BS, WIDTH * BS), F32),
            pltpu.VMEM((2, HALF, SPAN), BF16),
            pltpu.VMEM((2, HALF, SPAN), BF16),
            pltpu.VMEM((2, 5 * TILE, HALF), F32),
            pltpu.VMEM((2, 5 * TILE, HALF), F32),
            pltpu.VMEM((2, 5 * TILE, HALF), BF16),
            pltpu.VMEM((2, 5 * TILE, HALF), BF16),
            *[pltpu.VMEM((2, 2, HALF, HALF), F32)] * 7,
            pltpu.VMEM((2, 8, HALF), F32),
            pltpu.SemaphoreType.DMA((N_SEND,)),
            pltpu.SemaphoreType.DMA((N_RECV,)),
            pltpu.SemaphoreType.DMA(()),
        ],
        compiler_params=pltpu.CompilerParams(has_side_effects=True, vmem_limit_bytes=60 * 1024 * 1024),
    )(pattern, p_cov, a_blocks, q_diag.reshape(1, HALF))


def solution(mesh):
    return jax.shard_map(
        body,
        mesh=mesh,
        in_specs=(P("row", "col"), P("row", None, None, None), P("row", None), P("row")),
        out_specs=P("row", "col"),
        check_vma=False,
    )
```

```python
import jax
import jax.numpy as jnp
from jax import lax
from jax.experimental import pallas as pl
from jax.experimental.pallas import tpu as pltpu
from jax.sharding import PartitionSpec as P

BS = 128
REACH = 8
WIDTH = 2 * REACH + 1
HALF = 256
QUARTER = 64
TILE = 512
SPAN = (WIDTH + 1) * BS
MESH = pl.DeviceIdType.MESH
F32 = jnp.float32
BF16 = jnp.bfloat16

S_RELAYOUT, S_NOISE, S_BAND, S_FWD, S_HALO, S_MIRROR, S_BACK, N_SEND = 0, 4, 6, 8, 9, 41, 105, 109
R_RELAYOUT, R_NOISE, R_BAND, R_HALO, R_MIRROR, R_BACK, N_RECV = 0, 4, 6, 10, 42, 106, 110


def kernel(
    pattern_ref, p_ref, a_hbm, q_ref, o_ref,
    a_ref, own_noise, strip, band, band_hi, band_lo, ext_p, ext_k, ext_hi, ext_lo,
    first, first_m, first_t, total, total_m, total_t, result, noise, send, recv, load,
):
    row = lax.axis_index("row")
    col = lax.axis_index("col")
    x, z0, y = row % 4, (row // 4) % 2, row // 8
    core, zh = col % 2, col // 2
    j1 = (x + zh) % 2
    tile_i, tile_j = 4 * y + 2 * z0 + core, 4 * zh + 2 * j1 + x // 2

    def device(x, y, z0, zh, core):
        return (8 * y + 4 * z0 + x, 2 * zh + core)

    def remote(src, dst, target, s, r):
        return pltpu.make_async_remote_copy(
            src_ref=src, dst_ref=dst, send_sem=send.at[s], recv_sem=recv.at[r],
            device_id=target, device_id_type=MESH,
        )

    pending = []

    def start(src, dst, target, s, r, local=None):
        if local is True:
            pltpu.make_async_copy(src, dst, recv.at[r]).start()
            return
        copy = remote(src, dst, target, s, r)
        if local is None:
            copy.start()
            pending.append((None, copy))
            return
        pl.when(jnp.logical_not(local))(copy.start)
        pl.when(local)(pltpu.make_async_copy(src, dst, recv.at[r]).start)
        pending.append((jnp.logical_not(local), copy))

    def arrived(dst, r):
        remote(dst, dst, (row, col), 0, r).wait_recv()

    partner = device(x, y, z0, zh, 1 - core)

    a_load = pltpu.make_async_copy(a_hbm, a_ref, load)
    a_load.start()
    own_noise[...] = jnp.broadcast_to(q_ref[...], own_noise.shape)

    mine = x // 2 == core
    part = x % 2

    def strip_target(h):
        x_to = (core + zh) % 2 + 2 * h
        return device(x_to, y, z0, zh, x // 2), mine & (x_to == x)

    for cc in range(2):
        for h in range(2):
            target, local = strip_target(h)
            start(
                p_ref.at[:, pl.ds(TILE * h + HALF * cc, HALF)],
                ext_p.at[cc, pl.ds(pl.multiple_of(2 * TILE + HALF * part, HALF), HALF), :],
                target, S_RELAYOUT + 2 * cc + h, R_RELAYOUT + 2 * cc + part, local,
            )

    for h in range(2):
        target, local = strip_target(h)
        start(own_noise, noise.at[part], target, S_NOISE + h, R_NOISE + part, local)

    def right(x):
        return (x + 1) % 4

    def left(x):
        return (x + 3) % 4

    def split_band(c):
        for b in range(2):
            empty = slice(0, BS) if b else slice(WIDTH * BS, SPAN)
            rows = slice(b * BS, (b + 1) * BS)
            band_hi[c, rows, empty] = jnp.zeros((BS, BS), BF16)
            band_lo[c, rows, empty] = jnp.zeros((BS, BS), BF16)
            for d in range(WIDTH):
                value = band[c, b, :, d * BS:(d + 1) * BS]
                hi = value.astype(BF16)
                cols = slice((b + d) * BS, (b + d + 1) * BS)
                band_hi[c, rows, cols] = hi
                band_lo[c, rows, cols] = (value - hi.astype(F32)).astype(BF16)

    def block(b, d):
        wanted, slot = 2 * row + b + d - REACH, -1
        for s in range(pattern_ref.shape[1]):
            slot = jnp.where(pattern_ref[b, s] == wanted, s, slot)
        slot = jnp.where(wanted >= 0, slot, -1)
        return jnp.where(slot >= 0, a_ref[b, jnp.maximum(slot, 0)], 0.0)

    a_load.wait()
    for d in range(WIDTH):
        strip[:, d * BS:(d + 1) * BS] = block(core, d)
    for t, near_x in enumerate((right(x), left(x))):
        start(strip, band.at[part, core], device(near_x, y, z0, zh, x // 2),
              S_BAND + t, R_BAND + 2 * part + core)

    @pl.when(mine)
    def _():
        for b in range(2):
            for d in range(WIDTH):
                band[part, b, :, d * BS:(d + 1) * BS] = block(b, d)
        split_band(part)

    step = (x + 4 - 2 * core) % 4
    fwd_c = 1 - step % 2
    fwd_right = jnp.logical_or(step == 1, step == 2)
    fwd_b = jnp.where(fwd_right, 0, 1)
    fwd_x = jnp.where(fwd_right, right(x), left(x))

    def forward_band():
        unit = band.at[fwd_c, fwd_b]
        arrived(unit, R_BAND + 2 * fwd_c + fwd_b)
        fwd_copy.start()

    fwd_copy = remote(band.at[fwd_c, fwd_b], band.at[fwd_c, fwd_b],
                      device(fwd_x, y, z0, zh, core), S_FWD, R_BAND + 2 * fwd_c + fwd_b)
    pending.append((None, fwd_copy))

    d_slot = jnp.where(z0 == 0, 4, 0)
    y_slot = 4 - d_slot
    y_next = jnp.where(z0 == 0, (y + 1) % 4, (y + 3) % 4)
    near = jnp.where(core == 0, 1, 3)
    f_slot = jnp.where(core == 0, 4, 0)
    f_dst = jnp.where(core == 0, 3, 1)
    f_from_z = f_slot == d_slot

    def halo(ext, base):
        def at(v, slot):
            return ext.at[v // 2, pl.ds(pl.multiple_of(slot * TILE + HALF * (v % 2), HALF), HALF), :]

        def sem(kind, v):
            return 16 * base + 4 * kind + v

        def own(v):
            start(at(v, 2), at(v, y_slot), device(x, y, 1 - z0, zh, core),
                  S_HALO + sem(0, v), R_HALO + sem(0, v))
            start(at(v, 2), at(v, near), partner, S_HALO + sem(1, v), R_HALO + sem(1, v))

        def across(v):
            return remote(at(v, f_slot), at(v, f_dst), partner,
                          S_HALO + sem(3, v), R_HALO + sem(3, v))

        def from_z(v):
            arrived(at(v, d_slot), R_HALO + sem(0, v))
            start(at(v, d_slot), at(v, y_slot), device(x, y_next, z0, zh, core),
                  S_HALO + sem(2, v), R_HALO + sem(2, v))
            pl.when(f_from_z)(lambda: across(v).start())

        def from_y(v):
            arrived(at(v, y_slot), R_HALO + sem(2, v))
            pl.when(jnp.logical_not(f_from_z))(lambda: across(v).start())
            pending.append((None, across(v)))

        def rest(v):
            arrived(at(v, 4 - near), R_HALO + sem(1, v))
            arrived(at(v, 4 - f_dst), R_HALO + sem(3, v))

        return own, from_z, from_y, rest

    def split(ext, cc):
        def piece(n, _):
            rows = pl.ds(pl.multiple_of(n * BS, BS), BS)
            value = ext[cc, rows, :]
            hi = value.astype(BF16)
            ext_hi[cc, rows, :] = hi
            ext_lo[cc, rows, :] = (value - hi.astype(F32)).astype(BF16)
            return 0
        lax.fori_loop(0, 5 * TILE // BS, piece, 0)

    def product(c, cc):
        rows = pl.ds(pl.multiple_of(HALF * c, HALF), SPAN)
        hi, lo = ext_hi[cc, rows, :], ext_lo[cc, rows, :]
        acc = jnp.dot(band_hi[c], hi, preferred_element_type=F32)
        acc += jnp.dot(band_hi[c], lo, preferred_element_type=F32)
        acc += jnp.dot(band_lo[c], hi, preferred_element_type=F32)
        return acc

    def mirror(base, src, mid, dst):
        def quarter(ref, c, d, n):
            return ref.at[c, d, pl.ds(pl.multiple_of(n * QUARTER, QUARTER), QUARTER), :]

        def spread(c, d):
            base_s, base_r = S_MIRROR + 32 * base + 16 * c + 8 * d, R_MIRROR + 32 * base + 16 * c + 8 * d
            for n in (1, 3, 2, 0):
                r = (y + n) % 4
                start(quarter(src, c, d, r), quarter(mid, c, d, y), device(x, r, z0, zh, core),
                      base_s + n, base_r + y, None if n else True)

        def onward(c, d):
            base_s, base_r = S_MIRROR + 32 * base + 16 * c + 8 * d, R_MIRROR + 32 * base + 16 * c + 8 * d
            for n in (0, 1, 3, 2):
                r = (y + n) % 4
                unit = quarter(mid, c, d, r)
                arrived(unit, base_r + r)
                x_to = (z0 + r) % 2 + 2 * core
                here = (x == x_to) & (y == zh) & (z0 == j1) & (zh == r) & mine
                start(unit, quarter(dst, c, d, y), device(x_to, zh, j1, r, x // 2),
                      base_s + 4 + n, base_r + 4 + y, here)

        def landed(c, d):
            for r in range(4):
                arrived(quarter(dst, c, d, r), R_MIRROR + 32 * base + 16 * c + 8 * d + 4 + r)

        return spread, onward, landed

    on_diagonal = tile_i == tile_j
    eye = (
        lax.broadcasted_iota(jnp.int32, (HALF, HALF), 0)
        == lax.broadcasted_iota(jnp.int32, (HALF, HALF), 1)
    )

    def diagonal(c):
        values = jnp.broadcast_to(noise[c, 0:1, :], (HALF, HALF))
        return jnp.where(jnp.logical_and(eye, on_diagonal), values, 0.0)

    own, from_z, from_y, rest = halo(ext_p, 0)
    for v in range(4):
        arrived(ext_p.at[v // 2, pl.ds(2 * TILE + HALF * (v % 2), HALF), :], R_RELAYOUT + v)
        own(v)
    for n in range(5):
        if n < 4:
            from_z(n)
        if n > 0:
            from_y(n - 1)
    for cc in range(2):
        rest(2 * cc)
        rest(2 * cc + 1)
        split(ext_p, cc)
    for c in range(2):
        arrived(noise.at[c], R_NOISE + c)

    spread, onward, landed = mirror(0, first, first_m, first_t)
    other = jnp.logical_not(mine)
    soon = jnp.where((step == 1) | (step == 2), 1, 0)
    late = 1 - soon

    @pl.when(other)
    def _():
        forward_band()
        arrived(band.at[soon, 1 - fwd_b], R_BAND + 2 * soon + 1 - fwd_b)
        split_band(soon)

    for cc in range(2):
        first[soon, cc] = product(soon, cc)
        spread(soon, cc)
    pl.when(mine)(forward_band)
    onward(soon, 0)
    onward(soon, 1)
    pl.when(other)(lambda: arrived(band.at[late, fwd_b], R_BAND + 2 * late + fwd_b))
    arrived(band.at[late, 1 - fwd_b], R_BAND + 2 * late + 1 - fwd_b)
    split_band(late)
    for cc in range(2):
        first[late, cc] = product(late, cc)
        spread(late, cc)
    onward(late, 0)
    onward(late, 1)

    own, from_z, from_y, rest = halo(ext_k, 1)

    def combine(cc):
        for c in range(2):
            landed(cc, c)
            k = first[c, cc] + first_t[cc, c].T
            if c == cc:
                k += diagonal(c)
            ext_k[cc, 2 * TILE + HALF * c:2 * TILE + HALF * (c + 1), :] = k
            own(2 * cc + c)

    spread, onward, landed_total = mirror(1, total, total_m, total_t)

    def apply(cc):
        rest(2 * cc)
        rest(2 * cc + 1)
        split(ext_k, cc)
        for c in range(2):
            total[cc, c] = 0.25 * first[c, cc] + 0.03125 * product(c, cc)
            spread(cc, c)

    combine(0)
    combine(1)
    for n in range(4):
        from_z(n)
        if n > 0:
            from_y(n - 1)
    apply(0)
    from_y(3)
    onward(0, 0)
    onward(0, 1)
    apply(1)
    onward(1, 0)
    onward(1, 1)

    for c in range(2):
        target = device(2 * core + c, y, z0, zh, j1)
        local = (2 * core + c == x) & (j1 == core)
        for cc in range(2):
            landed_total(c, cc)
            p = ext_p[cc, 2 * TILE + HALF * c:2 * TILE + HALF * (c + 1), :]
            value = p + (total[cc, c] + total_t[c, cc].T)
            if c == cc:
                value += 0.25 * diagonal(c)
            result[c, cc] = value
            start(
                result.at[c, cc],
                o_ref.at[:, pl.ds(pl.multiple_of(TILE * (x // 2) + HALF * cc, HALF), HALF)],
                target, S_BACK + 2 * c + cc, R_BACK + 2 * (x // 2) + cc, local,
            )
    for h in range(2):
        for cc in range(2):
            arrived(o_ref.at[:, pl.ds(TILE * h + HALF * cc, HALF)], R_BACK + 2 * h + cc)

    for condition, copy in pending:
        if condition is None:
            copy.wait_send()
        else:
            pl.when(condition)(copy.wait_send)


def body(p_cov, a_blocks, pattern, q_diag):
    vmem = pl.BlockSpec(memory_space=pltpu.VMEM)
    return pl.pallas_call(
        kernel,
        out_shape=jax.ShapeDtypeStruct(p_cov.shape, F32),
        in_specs=[
            pl.BlockSpec(memory_space=pltpu.SMEM),
            pl.BlockSpec(memory_space=pl.ANY),
            pl.BlockSpec(memory_space=pl.ANY),
            vmem,
        ],
        out_specs=vmem,
        scratch_shapes=[
            pltpu.VMEM(a_blocks.shape, F32),
            pltpu.VMEM((8, HALF), F32),
            pltpu.VMEM((BS, WIDTH * BS), F32),
            pltpu.VMEM((2, 2, BS, WIDTH * BS), F32),
            pltpu.VMEM((2, HALF, SPAN), BF16),
            pltpu.VMEM((2, HALF, SPAN), BF16),
            pltpu.VMEM((2, 5 * TILE, HALF), F32),
            pltpu.VMEM((2, 5 * TILE, HALF), F32),
            pltpu.VMEM((2, 5 * TILE, HALF), BF16),
            pltpu.VMEM((2, 5 * TILE, HALF), BF16),
            *[pltpu.VMEM((2, 2, HALF, HALF), F32)] * 7,
            pltpu.VMEM((2, 8, HALF), F32),
            pltpu.SemaphoreType.DMA((N_SEND,)),
            pltpu.SemaphoreType.DMA((N_RECV,)),
            pltpu.SemaphoreType.DMA(()),
        ],
        compiler_params=pltpu.CompilerParams(has_side_effects=True, vmem_limit_bytes=60 * 1024 * 1024),
    )(pattern, p_cov, a_blocks, q_diag.reshape(1, HALF))


def solution(mesh):
    return jax.shard_map(
        body,
        mesh=mesh,
        in_specs=(P("row", "col"), P("row", None, None, None), P("row", None), P("row")),
        out_specs=P("row", "col"),
        check_vma=False,
    )
```

```python
import jax
import jax.numpy as jnp
from jax import lax
from jax.experimental import pallas as pl
from jax.experimental.pallas import tpu as pltpu
from jax.sharding import PartitionSpec as P

BS = 128
REACH = 8
WIDTH = 2 * REACH + 1
HALF = 256
QUARTER = 64
TILE = 512
SPAN = (WIDTH + 1) * BS
MESH = pl.DeviceIdType.MESH
F32 = jnp.float32
BF16 = jnp.bfloat16

S_RELAYOUT, S_NOISE, S_BAND, S_FWD, S_HALO, S_MIRROR, S_BACK, N_SEND = 0, 4, 6, 8, 9, 41, 105, 109
R_RELAYOUT, R_NOISE, R_BAND, R_HALO, R_MIRROR, R_BACK, N_RECV = 0, 4, 6, 10, 42, 106, 110


def kernel(
    pattern_ref, p_ref, a_hbm, q_ref, o_ref,
    a_ref, own_noise, strip, band, band_hi, band_lo, ext_p, ext_k, ext_hi, ext_lo,
    first, first_m, first_t, total, total_m, total_t, result, noise, send, recv, load,
):
    row = lax.axis_index("row")
    col = lax.axis_index("col")
    x, z0, y = row % 4, (row // 4) % 2, row // 8
    core, zh = col % 2, col // 2
    j1 = (x + zh) % 2
    tile_i, tile_j = 4 * y + 2 * z0 + core, 4 * zh + 2 * j1 + x // 2

    def device(x, y, z0, zh, core):
        return (8 * y + 4 * z0 + x, 2 * zh + core)

    def remote(src, dst, target, s, r):
        return pltpu.make_async_remote_copy(
            src_ref=src, dst_ref=dst, send_sem=send.at[s], recv_sem=recv.at[r],
            device_id=target, device_id_type=MESH,
        )

    pending = []

    def start(src, dst, target, s, r, local=None):
        if local is True:
            pltpu.make_async_copy(src, dst, recv.at[r]).start()
            return
        copy = remote(src, dst, target, s, r)
        if local is None:
            copy.start()
            pending.append((None, copy))
            return
        pl.when(jnp.logical_not(local))(copy.start)
        pl.when(local)(pltpu.make_async_copy(src, dst, recv.at[r]).start)
        pending.append((jnp.logical_not(local), copy))

    def arrived(dst, r):
        remote(dst, dst, (row, col), 0, r).wait_recv()

    partner = device(x, y, z0, zh, 1 - core)

    a_load = pltpu.make_async_copy(a_hbm, a_ref, load)
    a_load.start()
    own_noise[...] = jnp.broadcast_to(q_ref[...], own_noise.shape)

    mine = x // 2 == core
    part = x % 2

    def strip_target(h):
        x_to = (core + zh) % 2 + 2 * h
        return device(x_to, y, z0, zh, x // 2), mine & (x_to == x)

    for cc in range(2):
        for h in range(2):
            target, local = strip_target(h)
            start(
                p_ref.at[:, pl.ds(TILE * h + HALF * cc, HALF)],
                ext_p.at[cc, pl.ds(pl.multiple_of(2 * TILE + HALF * part, HALF), HALF), :],
                target, S_RELAYOUT + 2 * cc + h, R_RELAYOUT + 2 * cc + part, local,
            )

    for h in range(2):
        target, local = strip_target(h)
        start(own_noise, noise.at[part], target, S_NOISE + h, R_NOISE + part, local)

    def right(x):
        return (x + 1) % 4

    def left(x):
        return (x + 3) % 4

    def split_band(c):
        for b in range(2):
            empty = slice(0, BS) if b else slice(WIDTH * BS, SPAN)
            rows = slice(b * BS, (b + 1) * BS)
            band_hi[c, rows, empty] = jnp.zeros((BS, BS), BF16)
            band_lo[c, rows, empty] = jnp.zeros((BS, BS), BF16)
            for d in range(WIDTH):
                value = band[c, b, :, d * BS:(d + 1) * BS]
                hi = value.astype(BF16)
                cols = slice((b + d) * BS, (b + d + 1) * BS)
                band_hi[c, rows, cols] = hi
                band_lo[c, rows, cols] = (value - hi.astype(F32)).astype(BF16)

    def block(b, d):
        wanted, slot = 2 * row + b + d - REACH, -1
        for s in range(pattern_ref.shape[1]):
            slot = jnp.where(pattern_ref[b, s] == wanted, s, slot)
        slot = jnp.where(wanted >= 0, slot, -1)
        return jnp.where(slot >= 0, a_ref[b, jnp.maximum(slot, 0)], 0.0)

    a_load.wait()
    for d in range(WIDTH):
        strip[:, d * BS:(d + 1) * BS] = block(core, d)
    for t, near_x in enumerate((right(x), left(x))):
        start(strip, band.at[part, core], device(near_x, y, z0, zh, x // 2),
              S_BAND + t, R_BAND + 2 * part + core)

    @pl.when(mine)
    def _():
        for b in range(2):
            for d in range(WIDTH):
                band[part, b, :, d * BS:(d + 1) * BS] = block(b, d)
        split_band(part)

    step = (x + 4 - 2 * core) % 4
    fwd_c = 1 - step % 2
    fwd_right = jnp.logical_or(step == 1, step == 2)
    fwd_b = jnp.where(fwd_right, 0, 1)
    fwd_x = jnp.where(fwd_right, right(x), left(x))

    def forward_band():
        unit = band.at[fwd_c, fwd_b]
        arrived(unit, R_BAND + 2 * fwd_c + fwd_b)
        fwd_copy.start()

    fwd_copy = remote(band.at[fwd_c, fwd_b], band.at[fwd_c, fwd_b],
                      device(fwd_x, y, z0, zh, core), S_FWD, R_BAND + 2 * fwd_c + fwd_b)
    pending.append((None, fwd_copy))

    d_slot = jnp.where(z0 == 0, 4, 0)
    y_slot = 4 - d_slot
    y_next = jnp.where(z0 == 0, (y + 1) % 4, (y + 3) % 4)
    near = jnp.where(core == 0, 1, 3)
    f_slot = jnp.where(core == 0, 4, 0)
    f_dst = jnp.where(core == 0, 3, 1)
    f_from_z = f_slot == d_slot

    def halo(ext, base):
        def at(v, slot):
            return ext.at[v // 2, pl.ds(pl.multiple_of(slot * TILE + HALF * (v % 2), HALF), HALF), :]

        def sem(kind, v):
            return 16 * base + 4 * kind + v

        def own(v):
            start(at(v, 2), at(v, y_slot), device(x, y, 1 - z0, zh, core),
                  S_HALO + sem(0, v), R_HALO + sem(0, v))
            start(at(v, 2), at(v, near), partner, S_HALO + sem(1, v), R_HALO + sem(1, v))

        def across(v):
            return remote(at(v, f_slot), at(v, f_dst), partner,
                          S_HALO + sem(3, v), R_HALO + sem(3, v))

        def from_z(v):
            arrived(at(v, d_slot), R_HALO + sem(0, v))
            start(at(v, d_slot), at(v, y_slot), device(x, y_next, z0, zh, core),
                  S_HALO + sem(2, v), R_HALO + sem(2, v))
            pl.when(f_from_z)(lambda: across(v).start())

        def from_y(v):
            arrived(at(v, y_slot), R_HALO + sem(2, v))
            pl.when(jnp.logical_not(f_from_z))(lambda: across(v).start())
            pending.append((None, across(v)))

        def rest(v):
            arrived(at(v, 4 - near), R_HALO + sem(1, v))
            arrived(at(v, 4 - f_dst), R_HALO + sem(3, v))

        return own, from_z, from_y, rest

    def split(ext, cc):
        def piece(n, _):
            rows = pl.ds(pl.multiple_of(n * BS, BS), BS)
            value = ext[cc, rows, :]
            hi = value.astype(BF16)
            ext_hi[cc, rows, :] = hi
            ext_lo[cc, rows, :] = (value - hi.astype(F32)).astype(BF16)
            return 0
        lax.fori_loop(0, 5 * TILE // BS, piece, 0)

    def product(c, cc):
        rows = pl.ds(pl.multiple_of(HALF * c, HALF), SPAN)
        hi, lo = ext_hi[cc, rows, :], ext_lo[cc, rows, :]
        acc = jnp.dot(band_hi[c], hi, preferred_element_type=F32)
        acc += jnp.dot(band_hi[c], lo, preferred_element_type=F32)
        acc += jnp.dot(band_lo[c], hi, preferred_element_type=F32)
        return acc

    def mirror(base, src, mid, dst):
        def quarter(ref, c, d, n):
            return ref.at[c, d, pl.ds(pl.multiple_of(n * QUARTER, QUARTER), QUARTER), :]

        def spread(c, d):
            base_s, base_r = S_MIRROR + 32 * base + 16 * c + 8 * d, R_MIRROR + 32 * base + 16 * c + 8 * d
            for n in (0, 1, 3, 2):
                r = (y + n) % 4
                start(quarter(src, c, d, r), quarter(mid, c, d, y), device(x, r, z0, zh, core),
                      base_s + n, base_r + y, None if n else True)

        def onward(c, d):
            base_s, base_r = S_MIRROR + 32 * base + 16 * c + 8 * d, R_MIRROR + 32 * base + 16 * c + 8 * d
            for n in (0, 1, 3, 2):
                r = (y + n) % 4
                unit = quarter(mid, c, d, r)
                arrived(unit, base_r + r)
                x_to = (z0 + r) % 2 + 2 * core
                here = (x == x_to) & (y == zh) & (z0 == j1) & (zh == r) & mine
                start(unit, quarter(dst, c, d, y), device(x_to, zh, j1, r, x // 2),
                      base_s + 4 + n, base_r + 4 + y, here)

        def landed(c, d):
            for r in range(4):
                arrived(quarter(dst, c, d, r), R_MIRROR + 32 * base + 16 * c + 8 * d + 4 + r)

        return spread, onward, landed

    on_diagonal = tile_i == tile_j
    eye = (
        lax.broadcasted_iota(jnp.int32, (HALF, HALF), 0)
        == lax.broadcasted_iota(jnp.int32, (HALF, HALF), 1)
    )

    def diagonal(c):
        values = jnp.broadcast_to(noise[c, 0:1, :], (HALF, HALF))
        return jnp.where(jnp.logical_and(eye, on_diagonal), values, 0.0)

    own, from_z, from_y, rest = halo(ext_p, 0)
    for v in range(4):
        arrived(ext_p.at[v // 2, pl.ds(2 * TILE + HALF * (v % 2), HALF), :], R_RELAYOUT + v)
        own(v)
    for n in range(5):
        if n < 4:
            from_z(n)
        if n > 0:
            from_y(n - 1)
    for cc in range(2):
        rest(2 * cc)
        rest(2 * cc + 1)
        split(ext_p, cc)
    for c in range(2):
        arrived(noise.at[c], R_NOISE + c)

    spread, onward, landed = mirror(0, first, first_m, first_t)
    other = jnp.logical_not(mine)
    soon = jnp.where((step == 1) | (step == 2), 1, 0)
    late = 1 - soon

    @pl.when(other)
    def _():
        forward_band()
        arrived(band.at[soon, 1 - fwd_b], R_BAND + 2 * soon + 1 - fwd_b)
        split_band(soon)

    for cc in range(2):
        first[soon, cc] = product(soon, cc)
        spread(soon, cc)
    pl.when(mine)(forward_band)
    onward(soon, 0)
    onward(soon, 1)
    pl.when(other)(lambda: arrived(band.at[late, fwd_b], R_BAND + 2 * late + fwd_b))
    arrived(band.at[late, 1 - fwd_b], R_BAND + 2 * late + 1 - fwd_b)
    split_band(late)
    for cc in range(2):
        first[late, cc] = product(late, cc)
        spread(late, cc)
    onward(late, 0)
    onward(late, 1)

    own, from_z, from_y, rest = halo(ext_k, 1)

    def combine(cc):
        for c in range(2):
            landed(cc, c)
            k = first[c, cc] + first_t[cc, c].T
            if c == cc:
                k += diagonal(c)
            ext_k[cc, 2 * TILE + HALF * c:2 * TILE + HALF * (c + 1), :] = k
            own(2 * cc + c)

    spread, onward, landed_total = mirror(1, total, total_m, total_t)

    def apply(cc):
        rest(2 * cc)
        rest(2 * cc + 1)
        split(ext_k, cc)
        for c in range(2):
            total[cc, c] = 0.25 * first[c, cc] + 0.03125 * product(c, cc)
            spread(cc, c)

    combine(0)
    combine(1)
    for n in range(4):
        from_z(n)
        if n > 0:
            from_y(n - 1)
    apply(0)
    from_y(3)
    onward(0, 0)
    onward(0, 1)
    apply(1)
    onward(1, 0)
    onward(1, 1)

    for c in range(2):
        target = device(2 * core + c, y, z0, zh, j1)
        local = (2 * core + c == x) & (j1 == core)
        for cc in range(2):
            landed_total(c, cc)
            p = ext_p[cc, 2 * TILE + HALF * c:2 * TILE + HALF * (c + 1), :]
            value = p + (total[cc, c] + total_t[c, cc].T)
            if c == cc:
                value += 0.25 * diagonal(c)
            result[c, cc] = value
            start(
                result.at[c, cc],
                o_ref.at[:, pl.ds(pl.multiple_of(TILE * (x // 2) + HALF * cc, HALF), HALF)],
                target, S_BACK + 2 * c + cc, R_BACK + 2 * (x // 2) + cc, local,
            )
    for h in range(2):
        for cc in range(2):
            arrived(o_ref.at[:, pl.ds(TILE * h + HALF * cc, HALF)], R_BACK + 2 * h + cc)

    for condition, copy in pending:
        if condition is None:
            copy.wait_send()
        else:
            pl.when(condition)(copy.wait_send)


def body(p_cov, a_blocks, pattern, q_diag):
    vmem = pl.BlockSpec(memory_space=pltpu.VMEM)
    return pl.pallas_call(
        kernel,
        out_shape=jax.ShapeDtypeStruct(p_cov.shape, F32),
        in_specs=[
            pl.BlockSpec(memory_space=pltpu.SMEM),
            pl.BlockSpec(memory_space=pl.ANY),
            pl.BlockSpec(memory_space=pl.ANY),
            vmem,
        ],
        out_specs=pl.BlockSpec(memory_space=pl.ANY),
        scratch_shapes=[
            pltpu.VMEM(a_blocks.shape, F32),
            pltpu.VMEM((8, HALF), F32),
            pltpu.VMEM((BS, WIDTH * BS), F32),
            pltpu.VMEM((2, 2, BS, WIDTH * BS), F32),
            pltpu.VMEM((2, HALF, SPAN), BF16),
            pltpu.VMEM((2, HALF, SPAN), BF16),
            pltpu.VMEM((2, 5 * TILE, HALF), F32),
            pltpu.VMEM((2, 5 * TILE, HALF), F32),
            pltpu.VMEM((2, 5 * TILE, HALF), BF16),
            pltpu.VMEM((2, 5 * TILE, HALF), BF16),
            *[pltpu.VMEM((2, 2, HALF, HALF), F32)] * 7,
            pltpu.VMEM((2, 8, HALF), F32),
            pltpu.SemaphoreType.DMA((N_SEND,)),
            pltpu.SemaphoreType.DMA((N_RECV,)),
            pltpu.SemaphoreType.DMA(()),
        ],
        compiler_params=pltpu.CompilerParams(has_side_effects=True, vmem_limit_bytes=60 * 1024 * 1024),
    )(pattern, p_cov, a_blocks, q_diag.reshape(1, HALF))


def solution(mesh):
    return jax.shard_map(
        body,
        mesh=mesh,
        in_specs=(P("row", "col"), P("row", None, None, None), P("row", None), P("row")),
        out_specs=P("row", "col"),
        check_vma=False,
    )
```
